256 devices in a mesh: section: 4 (over z_lo), expert: 32 (over z_hi, y, x), dp: 2 (over core).
Axes of the slice: x: 4, y: 4, z: 8 (z_hi: 2, z_lo: 4; z = z_hi * 4 + z_lo), core: 2. Of those that a mesh axis runs over, the one named last changes fastest.
Arguments:
- x_fwd: bfloat16 [4, 4096, 3584], P('section', ('expert', 'dp')), may hold values from -6 to 6
- ids_fwd: int32 [4, 4096, 2], P('section', ('expert', 'dp')), may hold values from 0 to 7, all different within a row; in each aligned block of 64 rows (0 to 63, 64 to 127, ..., all dimensions but the last counted through in order) at most 20 rows name the same one
- route_fwd: float32 [4, 4096, 2], P('section', ('expert', 'dp')), may hold values from 0.1 to 1
- x_bwd: bfloat16 [4, 4096, 3584], P('section', ('expert', 'dp')), may hold values from -6 to 6
- ids_bwd: int32 [4, 4096, 2], P('section', ('expert', 'dp')), may hold values from 0 to 7, all different within a row; in each aligned block of 64 rows (0 to 63, 64 to 127, ..., all dimensions but the last counted through in order) at most 20 rows name the same one
- route_bwd: float32 [4, 4096, 2], P('section', ('expert', 'dp')), may hold values from 0.1 to 1
- dy_bwd: bfloat16 [4, 4096, 3584], P('section', ('expert', 'dp')), may hold values from -3 to 3
- w_gate: bfloat16 [4, 32, 3584, 256], P('section', 'expert', 'dp'), may hold values from -0.09375 to 0.09375
- w_up: bfloat16 [4, 32, 3584, 256], P('section', 'expert', 'dp'), may hold values from -0.09375 to 0.09375
- w_down: bfloat16 [4, 32, 256, 3584], P('section', 'expert', None, 'dp'), may hold values from -0.1875 to 0.1875
Outputs:
- y_next: bfloat16 [4, 4096, 3584], P('section', ('expert', 'dp'))
- dx_next: bfloat16 [4, 4096, 3584], P('section', ('expert', 'dp'))
- grad_gate: bfloat16 [4, 32, 3584, 256], P('section', 'expert', 'dp')
- grad_up: bfloat16 [4, 32, 3584, 256], P('section', 'expert', 'dp')
- grad_down: bfloat16 [4, 32, 256, 3584], P('section', 'expert', None, 'dp')
The draws below stay inside these ranges and needn't reach their ends.
Inputs may be any that keep to these rules, and one draw needn't show every extreme that they name: `ids_fwd`: each row names 2 different experts. In each aligned block of 64 rows of a section (the rows of one device) no expert is named by more than 20 rows, and in some block one expert is named by exactly 20 rows. `ids_bwd`: each row names 2 different experts. In each aligned block of 64 rows of a section (the rows of one device) no expert is named by more than 20 rows, and in some block one expert is named by exactly 20 rows.
All inputs are finite; a program needn't handle non-finite values.
Results may differ from the reference program's by a relative error of at most 0.0065.
Values may be sent and summed in bfloat16 or wider, within the bound.
A program may use at most 128 MiB of HBM per device.

```python
import math
import jax
import jax.numpy as jnp
import numpy as np
from jax import lax

D = 3584
FF = 1024
TOP = 2
TOK_DEV = 64
SECTIONS = 4
GROUP = 4
EXPERTS = 8
FS = 256
CAP = 20
MB = 4096
N_EXPERT = 32
N_DP = 2


def block_scale(own_key, extent, cuts, least, top_value):
    def one(dim, parts):
        draws = jax.random.uniform(jax.random.fold_in(jax.random.fold_in(own_key, 6), dim), (parts,), jnp.float32, least / len(cuts), top_value / len(cuts))
        return jnp.repeat(jnp.exp(draws), extent[dim] // parts).reshape((-1,) + (1,) * (len(extent) - dim - 1))

    level = one(*cuts[0])
    for cut in cuts[1:]:
        level = level * one(*cut)
    return level


def shared_out(key, own, number, rows, count, top, limit, lean):
    sequence = jax.random.permutation(key, count)
    heavy_load, usual = shares(count, rows * top, limit, lean, True), shares(count, rows * top, limit, lean, False)
    places = jnp.arange(count)

    def named(lengths, offset_by):
        used = int((lengths > 0).sum())
        fixed = max(1, used // 4)
        passed = fixed + (places - fixed + offset_by * (used - fixed)) % max(1, count - fixed)
        return jnp.zeros((count,), jnp.int32).at[sequence[jnp.where(places < fixed, places, passed)]].set(jnp.asarray(lengths, jnp.int32))

    lengths = jnp.where(number % 4 == 0, named(heavy_load, number // 4), named(usual, number - number // 4 - 1))
    mixed = jax.random.permutation(jax.random.fold_in(own, 3), count)
    source_of, taker = mixed[0:count // 2 * 2:2], mixed[1:count // 2 * 2:2]
    room = jnp.minimum(lengths[source_of] - 1, limit - lengths[taker]) // 2
    room = jnp.where((source_of == sequence[0]) | (taker == sequence[0]) | (lengths[taker] == 0), 0, jnp.maximum(room, 0))
    passed = jax.random.randint(jax.random.fold_in(own, 4), (count // 2,), 0, 1 << 20) % (room + 1)
    lengths = lengths.at[source_of].add(-passed).at[taker].add(passed)
    items = jnp.searchsorted(jnp.cumsum(lengths), jnp.arange(rows * top), side="right").astype(jnp.int32)
    listing = items.reshape(top, rows).T
    listing = listing[jax.random.permutation(jax.random.fold_in(own, 1), rows)]
    offset_by = jax.random.randint(jax.random.fold_in(own, 2), (rows, 1), 0, top)
    return jnp.take_along_axis(listing, (jnp.arange(top)[None, :] + offset_by) % top, axis=1)


def shares(count, total, reach, slope, full):
    loads = [(1 << 20) // math.isqrt(grade ** slope) + 1 for grade in range(1, count + 1)]
    largest = reach if full else min(reach, max(-(-total // count), total * loads[0] // sum(loads)))
    least = 1 if total - largest >= count - 1 else 0
    holding, spare = [largest] + [least] * (count - 1), total - largest - least * (count - 1)
    while spare > 0:
        free = [i for i in range(1, count) if holding[i] < largest] or [i for i in range(1, count) if holding[i] < reach]
        mass, remaining = sum([loads[i] for i in free]), spare
        for i in free:
            extra = min(reach - holding[i], max(1, remaining * loads[i] // mass), spare)
            holding[i] = holding[i] + extra
            spare = spare - extra
    return np.array(holding)


def centred(key, shape, deviation, bound, cuts=(), held_as=jnp.bfloat16):
    result = jax.random.normal(key, shape, jnp.float32) * deviation
    if len(cuts) > 0:
        result = block_scale(key, shape, cuts, -0.22, 0.18) * result
    return jnp.clip(result, min=-bound, max=bound).astype(held_as)


def setup_inputs(seed: int = 0) -> dict:
    arg_keys = jax.random.split(jax.random.key(seed), 11)
    x_fwd = centred(arg_keys[0], (SECTIONS, MB, D), 1.0, 6.0, ((0, 4), (1, 64)))
    ids_fwd_keys = jax.random.split(jax.random.fold_in(arg_keys[1], 1), SECTIONS * MB // TOK_DEV)
    ids_fwd_turns = jax.random.permutation(jax.random.fold_in(arg_keys[1], 3), SECTIONS * MB // TOK_DEV)
    ids_fwd = jax.vmap(lambda own, number: shared_out(jax.random.fold_in(arg_keys[1], 2), own, number, TOK_DEV, EXPERTS, TOP, CAP, 2))(ids_fwd_keys, ids_fwd_turns).reshape((SECTIONS, MB, TOP))
    route_fwd = jnp.clip(0.1 + 0.9 * jax.random.uniform(arg_keys[2], (SECTIONS, MB, TOP), jnp.float32) ** block_scale(arg_keys[2], (SECTIONS, MB, TOP), ((0, 4), (1, 64)), -0.2, 0.2), 0.1, 1.0)
    x_bwd = centred(arg_keys[3], (SECTIONS, MB, D), 1.0, 6.0, ((0, 4), (1, 64)))
    ids_bwd_keys = jax.random.split(jax.random.fold_in(arg_keys[4], 1), SECTIONS * MB // TOK_DEV)
    ids_bwd_turns = jax.random.permutation(jax.random.fold_in(arg_keys[4], 3), SECTIONS * MB // TOK_DEV)
    ids_bwd = jax.vmap(lambda own, number: shared_out(jax.random.fold_in(arg_keys[4], 2), own, number, TOK_DEV, EXPERTS, TOP, CAP, 2))(ids_bwd_keys, ids_bwd_turns).reshape((SECTIONS, MB, TOP))
    route_bwd = jnp.clip(0.1 + 0.9 * jax.random.uniform(arg_keys[5], (SECTIONS, MB, TOP), jnp.float32) ** block_scale(arg_keys[5], (SECTIONS, MB, TOP), ((0, 4), (1, 64)), -0.2, 0.2), 0.1, 1.0)
    dy_bwd = centred(arg_keys[6], (SECTIONS, MB, D), 0.5, 3.0, ((0, 4), (1, 64)))
    w_gate = centred(arg_keys[7], (SECTIONS, EXPERTS * GROUP, D, FS), D ** -0.5, 0.09375, ((0, 4), (1, 32), (2, 2)))
    w_up = centred(arg_keys[8], (SECTIONS, EXPERTS * GROUP, D, FS), D ** -0.5, 0.09375, ((0, 4), (1, 32), (2, 2)))
    w_down = centred(arg_keys[9], (SECTIONS, EXPERTS * GROUP, FS, D), FF ** -0.5, 0.1875, ((0, 4), (1, 32), (3, 2)))
    return dict(x_fwd=x_fwd, ids_fwd=ids_fwd, route_fwd=route_fwd, x_bwd=x_bwd, ids_bwd=ids_bwd, route_bwd=route_bwd, dy_bwd=dy_bwd, w_gate=w_gate, w_up=w_up, w_down=w_down)


def pair_positions(ids):
    blocks = ids.shape[0] // TOK_DEV
    flat = ids.reshape(blocks, TOK_DEV * TOP)
    onehot = (flat[:, :, None] == jnp.arange(EXPERTS, dtype=jnp.int32)[None, None, :]).astype(jnp.int32)
    position = jnp.sum(jnp.cumsum(onehot, axis=1) * onehot, axis=2) - 1
    block_base = (jnp.arange(blocks, dtype=jnp.int32) * CAP)[:, None]
    return (block_base + position).astype(jnp.int32).reshape(ids.shape[0], TOP)


def gather_rows(values, target, slot_total):
    buffer = jnp.zeros((slot_total + 1, values.shape[1]), values.dtype)
    return buffer.at[target].set(values)[:slot_total]


def slab_sum(products):
    total = None
    for left, right in products:
        term = jnp.einsum("rgf,gfd->grd", left.reshape(left.shape[0], GROUP, FS).astype(jnp.float32), right.astype(jnp.float32), precision=lax.Precision.HIGHEST)
        total = term if total is None else total + term
    rounded = lax.optimization_barrier(total.astype(jnp.bfloat16))
    return jnp.sum(rounded.astype(jnp.float32), axis=0)


def data_reduce(left, right):
    left_split = left.reshape(N_EXPERT, N_DP, CAP, left.shape[1]).astype(jnp.float32)
    right_split = right.reshape(N_EXPERT, N_DP, CAP, right.shape[1]).astype(jnp.float32)
    halves = jnp.einsum("sdca,sdcb->dab", left_split, right_split, precision=lax.Precision.HIGHEST)
    rounded = lax.optimization_barrier(halves.astype(jnp.bfloat16))
    return jnp.sum(rounded.astype(jnp.float32), axis=0).astype(jnp.bfloat16)


def section_forward(inputs):
    x_rows, ids, route, w_gate, w_up, w_down = inputs
    slot_total = (ids.shape[0] // TOK_DEV) * CAP
    destination = pair_positions(ids)
    pair_rows = jnp.repeat(x_rows, TOP, axis=0)
    gate_slabs = w_gate.reshape(EXPERTS, GROUP, D, FS)
    up_slabs = w_up.reshape(EXPERTS, GROUP, D, FS)
    down_slabs = w_down.reshape(EXPERTS, GROUP, FS, D)

    def one_expert(accumulated, items):
        expert_id, gate_w, up_w, down_w = items
        expert_mask = ids == expert_id
        target = jnp.where(expert_mask, destination, slot_total).reshape(-1)
        expert_rows = gather_rows(pair_rows, target, slot_total)
        gate_pre = jnp.dot(expert_rows, gate_w.transpose(1, 0, 2).reshape(D, FF), preferred_element_type=jnp.float32)
        up_proj = jnp.dot(expert_rows, up_w.transpose(1, 0, 2).reshape(D, FF), preferred_element_type=jnp.float32)
        hidden = (jax.nn.silu(gate_pre) * up_proj).astype(jnp.bfloat16)
        output = slab_sum([(hidden, down_w)])
        picked = output[jnp.minimum(target, slot_total - 1)].reshape(ids.shape[0], TOP, D)
        weighted = jnp.where(expert_mask[:, :, None], route[:, :, None] * picked, 0.0)
        return accumulated + jnp.sum(weighted, axis=1), None

    start = jnp.zeros((ids.shape[0], D), jnp.float32)
    total, _ = lax.scan(one_expert, start, (jnp.arange(EXPERTS, dtype=jnp.int32), gate_slabs, up_slabs, down_slabs))
    return total.astype(jnp.bfloat16)


def section_backward(inputs):
    x_rows, ids, route, dy_rows, w_gate, w_up, w_down = inputs
    slot_total = (ids.shape[0] // TOK_DEV) * CAP
    destination = pair_positions(ids)
    pair_rows = jnp.repeat(x_rows, TOP, axis=0)
    cotangent = (route[:, :, None] * dy_rows[:, None, :].astype(jnp.float32)).astype(jnp.bfloat16).reshape(-1, D)
    gate_slabs = w_gate.reshape(EXPERTS, GROUP, D, FS)
    up_slabs = w_up.reshape(EXPERTS, GROUP, D, FS)
    down_slabs = w_down.reshape(EXPERTS, GROUP, FS, D)

    def one_expert(accumulated, items):
        expert_id, gate_w, up_w, down_w = items
        expert_mask = ids == expert_id
        target = jnp.where(expert_mask, destination, slot_total).reshape(-1)
        expert_rows = gather_rows(pair_rows, target, slot_total)
        expert_cot = gather_rows(cotangent, target, slot_total)
        gate_pre = jnp.dot(expert_rows, gate_w.transpose(1, 0, 2).reshape(D, FF), preferred_element_type=jnp.float32)
        up_proj = jnp.dot(expert_rows, up_w.transpose(1, 0, 2).reshape(D, FF), preferred_element_type=jnp.float32)
        sigmoid_gate = jax.nn.sigmoid(gate_pre)
        activated = gate_pre * sigmoid_gate
        hidden = (activated * up_proj).astype(jnp.bfloat16)
        d_hidden = jnp.dot(expert_cot, down_w.reshape(FF, D).T, preferred_element_type=jnp.float32)
        d_up = (d_hidden * activated).astype(jnp.bfloat16)
        d_gate = (d_hidden * up_proj * sigmoid_gate * (1.0 + gate_pre * (1.0 - sigmoid_gate))).astype(jnp.bfloat16)
        back = slab_sum([(d_gate, gate_w.transpose(0, 2, 1)), (d_up, up_w.transpose(0, 2, 1))])
        picked = back[jnp.minimum(target, slot_total - 1)].reshape(ids.shape[0], TOP, D)
        summed = jnp.sum(jnp.where(expert_mask[:, :, None], picked, 0.0), axis=1)
        grad_g = data_reduce(expert_rows, d_gate).reshape(D, GROUP, FS).transpose(1, 0, 2)
        grad_u = data_reduce(expert_rows, d_up).reshape(D, GROUP, FS).transpose(1, 0, 2)
        grad_d = data_reduce(hidden, expert_cot).reshape(GROUP, FS, D)
        return accumulated + summed, (grad_g, grad_u, grad_d)

    start = jnp.zeros((ids.shape[0], D), jnp.float32)
    total, grads = lax.scan(one_expert, start, (jnp.arange(EXPERTS, dtype=jnp.int32), gate_slabs, up_slabs, down_slabs))
    grad_g = grads[0].reshape(EXPERTS * GROUP, D, FS)
    grad_u = grads[1].reshape(EXPERTS * GROUP, D, FS)
    grad_d = grads[2].reshape(EXPERTS * GROUP, FS, D)
    return total.astype(jnp.bfloat16), grad_g, grad_u, grad_d


def reference(x_fwd, ids_fwd, route_fwd, x_bwd, ids_bwd, route_bwd, dy_bwd, w_gate, w_up, w_down):
    outputs = lax.map(section_forward, (x_fwd, ids_fwd, route_fwd, w_gate, w_up, w_down))
    back, grad_gate, grad_up, grad_down = lax.map(section_backward, (x_bwd, ids_bwd, route_bwd, dy_bwd, w_gate, w_up, w_down))
    y_next = jnp.roll(outputs, 1, axis=0)
    dx_next = jnp.roll(back, 1, axis=0)
    return y_next, dx_next, grad_gate, grad_up, grad_down
```

```python
import jax
import jax.numpy as jnp
from jax import lax
from jax.sharding import PartitionSpec as P

FF = 1024
TOP = 2
BF = jnp.bfloat16
F32 = jnp.float32


def dot(left, right):
    return jnp.dot(left, right, preferred_element_type=F32)


def contract_first(left, right):
    return lax.dot_general(left, right, (((0,), (0,)), ((), ())), preferred_element_type=F32)


def contract_last(left, right):
    return lax.dot_general(left, right, (((1,), (1,)), ((), ())), preferred_element_type=F32)


def along_expert(value, move):
    return lax.ppermute(value, "expert", [(e, move(e)) for e in range(32)])


def to_mirror(value):
    return along_expert(value, lambda e: e ^ 16)


def to_y(value, steps):
    return along_expert(value, lambda e: (e & 19) | ((((e >> 2) + steps) & 3) << 2))


def to_row_partner(value):
    return along_expert(value, lambda e: e ^ 1)


def to_slab_partner(value):
    return along_expert(value, lambda e: e ^ 3 if (e & 3) in (0, 3) else (e & ~3) | (3 - (e & 3)))


def to_core(value):
    return lax.ppermute(value, "dp", [(0, 1), (1, 0)])


def to_next_section(value, mirror):
    pairs = [
        (s * 32 + e, ((s + 1) % 4) * 32 + (e ^ 16 if mirror else e)) for s in range(4) for e in range(32)
    ]
    return lax.ppermute(value, ("section", "expert"), pairs)


def rotate(value, core):
    half = value.shape[-1] // 2
    turned = jnp.concatenate([value[..., half:], value[..., :half]], axis=-1)
    return jnp.where(core == 0, value, turned)


def pair_slots(ids, half, my_y, room):
    key = jnp.where((ids >> 2) == half, (ids - my_y) & 3, -1)
    count = key.shape[-1]
    earlier = jnp.arange(count)[None, :, None] > jnp.arange(count)[None, None, :]
    same = (key[:, :, None] == key[:, None, :]) & earlier
    position = jnp.sum(same.astype(jnp.int32), axis=2)
    block = jnp.arange(key.shape[0], dtype=jnp.int32)[:, None] & 1
    return jnp.where(key >= 0, key * (2 * room) + block * room + position, -1)


def exchange_y(value, sign):
    block = value.shape[0] // 4
    parts = [value[d * block:(d + 1) * block] for d in range(4)]
    one, three = to_y(parts[1], sign), to_y(parts[3], -sign)
    two = to_y(parts[2], 2)
    return jnp.concatenate([parts[0], one, two, three], axis=0)


def local(x_fwd, ids_fwd, route_fwd, x_bwd, ids_bwd, route_bwd, dy_bwd, w_gate, w_up, w_down):
    expert = lax.axis_index("expert")
    core = lax.axis_index("dp")
    half, my_y = expert >> 4, (expert >> 2) & 3
    rows, width = x_fwd.shape[1], x_fwd.shape[2]
    wide = width // 2
    slab = w_gate.shape[-1]
    room = 20
    slots = 8 * room

    info = jnp.concatenate(
        [ids_bwd[0].astype(F32), ids_fwd[0].astype(F32), route_bwd[0], route_fwd[0]], axis=1
    )
    far_info = to_mirror(info)
    xb, dy, xf = rotate(x_bwd[0], core), rotate(dy_bwd[0], core), rotate(x_fwd[0], core)
    xb_far = to_mirror(xb)
    dy_far = to_mirror(dy)
    xf_far = to_mirror(xf)
    wg_part, wu_part, wd_part = w_gate[0, 0], w_up[0, 0], w_down[0, 0]
    wg_x, wu_x, wd_x = to_slab_partner(wg_part), to_slab_partner(wu_part), to_slab_partner(wd_part)

    both = jnp.stack([info, far_info], axis=0)
    ids = both[:, :, :4].astype(jnp.int32)
    key_b = ids[:, :, :2].reshape(2, rows * TOP)
    key_f = ids[:, :, 2:].reshape(2, rows * TOP)
    slot = pair_slots(jnp.concatenate([key_b, key_f], axis=0), half, my_y, room)
    slot_b = slot[:2].reshape(2 * rows, TOP)
    slot_f = slot[2:].reshape(2 * rows, TOP)
    route_b = both[:, :, 4:6].reshape(2 * rows, TOP)
    route_f = both[:, :, 6:8].reshape(2 * rows, TOP)
    line = jnp.arange(slots, dtype=jnp.int32)
    hit_b = slot_b[:, :, None] == line
    hit_f = slot_f[:, :, None] == line
    pick_b = jnp.any(hit_b, axis=1).astype(BF)
    pick_f = jnp.any(hit_f, axis=1).astype(BF)
    weight_b = jnp.sum(jnp.where(hit_b, route_b[:, :, None], 0.0), axis=(0, 1))
    weight_f = jnp.sum(jnp.where(hit_f, route_f[:, :, None], 0.0), axis=1)

    wg_wide = jnp.concatenate([wg_part, wg_x], axis=1)
    wu_wide = jnp.concatenate([wu_part, wu_x], axis=1)
    wd_wide = jnp.concatenate([wd_part, wd_x], axis=0)
    wg = jnp.concatenate([wg_wide, to_core(wg_wide)], axis=0)
    wu = jnp.concatenate([wu_wide, to_core(wu_wide)], axis=0)
    wd = jnp.concatenate([wd_wide, to_core(wd_wide)], axis=1)

    send_b = contract_first(pick_b, jnp.concatenate([xb, xb_far], axis=0)).astype(BF)
    here_b = exchange_y(send_b, 1)
    there_b = to_row_partner(here_b)
    send_g = contract_first(pick_b, jnp.concatenate([dy, dy_far], axis=0))
    send_g = (send_g * weight_b[:, None]).astype(BF)
    here_g = exchange_y(send_g, 1)
    there_g = to_row_partner(here_g)
    send_f = contract_first(pick_f, jnp.concatenate([xf, xf_far], axis=0)).astype(BF)
    here_f = exchange_y(send_f, 1)
    there_f = to_row_partner(here_f)

    rows_b = jnp.concatenate([there_b, here_b], axis=0)
    cot = jnp.concatenate([there_g, here_g], axis=0)
    gate_b, up_b = dot(rows_b, wg), dot(rows_b, wu)
    sig = jax.nn.sigmoid(gate_b)
    act = gate_b * sig
    hid_b = (act * up_b).astype(BF)
    d_hid = contract_last(cot, wd)
    d_up = (d_hid * act).astype(BF)
    d_gate = (d_hid * up_b * sig * (1.0 + gate_b * (1.0 - sig))).astype(BF)

    back_away = (contract_last(d_gate[:slots], wg) + contract_last(d_up[:slots], wu)).astype(BF)
    back_in = to_row_partner(back_away)

    grad_sets = []
    for left, right, axis in ((hid_b, cot, 1), (rows_b, d_gate, 0), (rows_b, d_up, 0)):
        if axis == 0:
            away = contract_first(left[:, wide:], right).astype(BF)
        else:
            away = contract_first(left, right[:, wide:]).astype(BF)
        grad_sets.append((left, right, axis, to_core(away)))
    grads = []
    for left, right, axis, core_in in grad_sets:
        if axis == 0:
            near = left[:, :wide]
            give = (contract_first(near, right[:, slab:]) + core_in[:, slab:].astype(F32)).astype(BF)
            keep = contract_first(near, right[:, :slab]) + core_in[:, :slab].astype(F32)
        else:
            near = right[:, :wide]
            give = (contract_first(left[:, slab:], near) + core_in[slab:].astype(F32)).astype(BF)
            keep = contract_first(left[:, :slab], near) + core_in[:slab].astype(F32)
        grads.append((keep + to_slab_partner(give).astype(F32)).astype(BF))
    grad_down, grad_gate, grad_up = grads

    back_here = contract_last(d_gate[slots:], wg) + contract_last(d_up[slots:], wu)
    back_here = (back_here + back_in.astype(F32)).astype(BF)
    home_b = exchange_y(back_here, -1)
    sum_b = dot(pick_b, home_b).astype(BF)
    dx = to_next_section(sum_b[rows:], True).astype(F32) + to_next_section(sum_b[:rows], False).astype(F32)
    dx_next = rotate(dx.astype(BF), core)

    rows_f = jnp.concatenate([there_f, here_f], axis=0)
    hid_f = (jax.nn.silu(dot(rows_f, wg)) * dot(rows_f, wu)).astype(BF)
    out_in = to_row_partner(dot(hid_f[:slots], wd).astype(BF))
    out_here = (dot(hid_f[slots:], wd) + out_in.astype(F32)).astype(BF)
    home_f = exchange_y(out_here, -1)
    high = weight_f.astype(BF)
    low = (weight_f - high.astype(F32)).astype(BF)
    sum_f = (dot(high, home_f) + dot(low, home_f)).astype(BF)
    out = to_next_section(sum_f[rows:], True).astype(F32) + to_next_section(sum_f[:rows], False).astype(F32)
    y_next = rotate(out.astype(BF), core)

    return (
        y_next[None],
        dx_next[None],
        grad_gate[None, None],
        grad_up[None, None],
        grad_down[None, None],
    )


def solution(mesh):
    tokens = P("section", ("expert", "dp"), None)
    tall = P("section", "expert", "dp", None)
    broad = P("section", "expert", None, "dp")
    return jax.shard_map(
        local,
        mesh=mesh,
        in_specs=(tokens,) * 7 + (tall, tall, broad),
        out_specs=(tokens, tokens, tall, tall, broad),
        check_vma=False,
    )
```
